32 devices in a mesh: macro: 8 (over z, y), pencil: 4 (over x, core).
Axes of the slice: x: 2, y: 2, z: 4, core: 2. Of those that a mesh axis runs over, the one named last changes fastest.
Arguments:
- voxel_material_ids: int32 [8, 128, 128, 128], P('macro', 'pencil'), may hold values from 0 to 2
- fiber_fraction: float32 [8, 128, 128, 128], P('macro', 'pencil'), may hold values from 0.5 to 18, as said below
- material_matrix_diffusivity: float32 [8, 3], P('macro'), may hold values from 0.2 to 5
- mesh_point_thermal_state: float32 [32], P('macro'), may hold values from 0.5 to 1.5
- element_corner_ids: int32 [8, 8], P('macro'), may hold values from 0 to 31, all different within a row
- global_entry_position: int32 [32], P('macro'), may hold values from 0 to 31, each once
- sample_choice_per_point: int32 [8], P('macro'), may hold values from 0 to 7, as said below
Outputs:
- qp_flux: float32 [8, 3], P('macro')
- nodal_flux: float32 [32], P('macro')
The draws below stay inside these ranges and needn't reach their ends.
Inputs may be any that keep to these rules, and one draw needn't show every extreme that they name: `fiber_fraction`: positive. `sample_choice_per_point`: exactly 2 microstructures are used by 2 points each, 4 by 1 points each, and the rest by none.
All inputs are finite; a program needn't handle non-finite values.
Results may differ from the reference program's by a relative error of at most 0.0003.
Values sent between devices are 32-bit elements; how exact they have to be, the bound alone decides.
A program may use at most 64 MiB of HBM per device.

```python
import math
import jax
import jax.numpy as jnp
from jax import lax

NV = 128
PHASES = 3
ITERS = 2
QP_DEV = 1
MICRO = 8
QPS = 8
GLOBAL_MESH_PTS = 32


def draw_fiber_fraction(key, part):
    key_base, key_cols = jax.random.split(jax.random.fold_in(key, 7))
    shape = (MICRO, NV, NV, NV)
    base = jnp.exp(jax.random.uniform(key_base, shape, jnp.float32, math.log(0.5), math.log(2.0)))
    cols = jnp.exp(jax.random.uniform(key_cols, (MICRO, 1, NV, 1), jnp.float32, 0.0, math.log(3.0)))
    ramp = jnp.exp(math.log(3.0) * jnp.arange(NV).astype(jnp.float32) / (NV - 1)).reshape(1, NV, 1, 1)
    return (base * cols * ramp).astype(jnp.float32)


def draw_sample_choice_per_point(key, part):
    key_groups, key_points = jax.random.split(jax.random.fold_in(key, 11))
    order = jax.random.permutation(key_groups, MICRO)
    places = jnp.arange(QPS)
    quarter = MICRO // 4
    heavy_index = jnp.clip(places // (2 * QP_DEV), 0, quarter - 1)
    light_index = jnp.clip(quarter + (places - QPS // 2) // QP_DEV, 0, MICRO - 1)
    group = jnp.where(places < QPS // 2, order[heavy_index], order[light_index])
    return jax.random.permutation(key_points, group).astype(jnp.int32)


def place_ends(values, own_key, smallest, high):
    place = [jax.random.randint(jax.random.fold_in(own_key, axis), (), 0, length) for axis, length in enumerate(values.shape)]
    main_axis = values.shape.index(max(values.shape))
    neighbour = place[:main_axis] + [(place[main_axis] + 1) % values.shape[main_axis]] + place[main_axis + 1:]
    return values.at[tuple(place)].set(smallest).at[tuple(neighbour)].set(high)


def block_levels(stream_key, dims, cuts, smallest, largest):
    gain, own = 1.0, jax.random.fold_in(stream_key, 6)
    for axis_at, blocks in cuts:
        steps = jnp.exp(jax.random.uniform(jax.random.fold_in(own, axis_at), (blocks,), jnp.float32, smallest / len(cuts), largest / len(cuts)))
        gain = gain * jnp.repeat(steps, dims[axis_at] // blocks).reshape([-1 if axis == axis_at else 1 for axis in range(len(dims))])
    return gain


def choose_distinct(stream_key, rows, count, top, lift):
    sequence = jax.random.permutation(jax.random.fold_in(stream_key, 1), count)
    favour = sequence
    for power in range(3):
        favour = favour * favour // count
    favour = favour * lift // count
    tickets = jax.random.randint(jax.random.fold_in(stream_key, 2), (rows, count), 0, 4096) + favour
    fixed_rows = jax.random.permutation(jax.random.fold_in(stream_key, 3), rows)[jnp.arange(count) % rows]
    tickets = jnp.where(jnp.arange(rows)[:, None] == fixed_rows[None, :], 1 << 14, tickets)
    merit = tickets * count + jnp.arange(count)
    return lax.top_k(merit.astype(jnp.int32), top)[1].astype(jnp.int32)


def setup_inputs(seed: int = 0) -> dict:
    streams_of = jax.random.split(jax.random.key(seed), 8)
    return {
        "voxel_material_ids": place_ends(jax.random.randint(streams_of[0], (MICRO, NV, NV, NV), 0, PHASES), jax.random.fold_in(streams_of[0], 1), 0, PHASES - 1).astype(jnp.int32),
        "fiber_fraction": draw_fiber_fraction(jax.random.fold_in(streams_of[7], 71), 0),
        "material_matrix_diffusivity": jnp.clip(jnp.exp(math.log(5.0) - 3.218876 * jax.random.uniform(streams_of[2], (MICRO, PHASES), jnp.float32) ** block_levels(streams_of[2], (MICRO, PHASES), ((0, 8),), -0.2, 0.2)), 0.2, 5.0),
        "mesh_point_thermal_state": jnp.clip(0.5 + 1.0 * jax.random.uniform(streams_of[3], (GLOBAL_MESH_PTS,), jnp.float32) ** block_levels(streams_of[3], (GLOBAL_MESH_PTS,), ((0, 8),), -0.2, 0.2), 0.5, 1.5),
        "element_corner_ids": choose_distinct(streams_of[4], QPS, GLOBAL_MESH_PTS, 8, 0),
        "global_entry_position": jax.random.permutation(streams_of[5], GLOBAL_MESH_PTS).astype(jnp.int32),
        "sample_choice_per_point": draw_sample_choice_per_point(jax.random.fold_in(streams_of[7], 71), 0),
    }


HIGHEST = lax.Precision.HIGHEST

def corner_signs():
    table = [[2.0 * (corner >> device_axis & 1) - 1.0 for device_axis in range(3)] for corner in range(8)]
    return jnp.array(table, dtype=jnp.float32)

def base_field(voxel_material_ids, fiber_fraction, material_matrix_diffusivity):
    conduct = jnp.zeros(fiber_fraction.shape, jnp.float32)
    for phase in range(PHASES):
        column = material_matrix_diffusivity[:, phase][:, None, None, None]
        conduct = conduct + jnp.where(voxel_material_ids == phase, column, 0.0)
    return conduct * fiber_fraction

def solve_point(conduct, gradient, heat):
    field = conduct + heat ** 3
    reference_k = jnp.sqrt(jnp.mean(field * field))
    modes = jnp.arange(NV).astype(jnp.float32)
    line = 4.0 * jnp.sin(math.pi * modes / NV) ** 2
    eigen = line[:, None, None] + line[None, :, None] + line[None, None, :]
    positive = eigen > 0
    weight = jnp.where(positive, 1.0 / (reference_k * jnp.where(positive, eigen, 1.0)), 0.0)
    gradient_field = [gradient[device_axis] + jnp.zeros_like(field) for device_axis in range(3)]
    for sweep in range(ITERS):
        source = jnp.zeros_like(field)
        for device_axis in range(3):
            polar = (field - reference_k) * gradient_field[device_axis]
            source = source + polar - jnp.roll(polar, 1, axis=device_axis)
        potential = jnp.real(jnp.fft.ifftn(jnp.fft.fftn(source) * weight))
        gradient_field = [gradient[device_axis] + jnp.roll(potential, -1, axis=device_axis) - potential for device_axis in range(3)]
    return jnp.stack([jnp.mean(field * gradient_field[device_axis]) for device_axis in range(3)])

def reference(voxel_material_ids, fiber_fraction, material_matrix_diffusivity, mesh_point_thermal_state, element_corner_ids, global_entry_position, sample_choice_per_point):
    signs = corner_signs()
    fourier_argument = mesh_point_thermal_state[element_corner_ids]
    gradient = jnp.dot(fourier_argument, signs, precision=HIGHEST) / 4.0
    heat = lax.optimization_barrier(jnp.sum(fourier_argument, axis=1)) / 8.0
    conduct = base_field(voxel_material_ids, fiber_fraction, material_matrix_diffusivity)

    def one_point(packed):
        point_gradient, point_heat, group = packed
        chosen = lax.dynamic_index_in_dim(conduct, group, 0, keepdims=False)
        return solve_point(chosen, point_gradient, point_heat)
    qp_flux = lax.map(one_point, (gradient, heat, sample_choice_per_point))
    residual = jnp.dot(qp_flux, signs.T, precision=HIGHEST) / 4.0
    rows = global_entry_position[element_corner_ids]
    nodal_flux = jnp.zeros((GLOBAL_MESH_PTS,), jnp.float32).at[rows.reshape(-1)].add(residual.reshape(-1))
    return (qp_flux, nodal_flux)
```

```python
import functools
import math

import jax
import jax.numpy as jnp
import numpy as np
from jax import lax
from jax.experimental import pallas as pl
from jax.experimental.pallas import tpu as pltpu
from jax.sharding import PartitionSpec as P

PHASES = 3
MESH = pl.DeviceIdType.MESH
F32 = jnp.float32
BF16 = jnp.bfloat16
GROUP = 4
STATS = 16
PAD = 8
BLOCK = 32


def hartley_tables(width):
    index = np.arange(width)
    angle = 2.0 * math.pi / width * (index[:, None] * index[None, :] % width)
    table = np.cos(angle) + np.sin(angle)
    high = table.astype(BF16)
    low = (table - high.astype(np.float64)).astype(BF16)
    right = np.concatenate([np.concatenate([high, low], axis=1)] * 2, axis=0)
    return right, np.ascontiguousarray(right.T)


def mode_tables(width, slab):
    line = 4.0 * np.sin(math.pi * np.arange(width) / width) ** 2
    lam = line[:, None] + line[None, :]
    safe = np.where(lam > 0, lam, 1.0)
    half = 1.0 + safe / 2.0
    root = half - np.sqrt(half * half - 1.0)
    scale = 1.0 / (1.0 / root - root) / width**2
    root[0, 0] = 1.0
    scale[0, 0] = 1.0 / width**3
    closing = 1.0 / (1.0 - np.where(lam > 0, root**width, 0.0))
    closing[0, 0] = 0.0
    return np.stack([root, scale, root**slab, closing]).astype(np.float32)


def split(x):
    high = x.astype(BF16)
    return high, (x - high.astype(F32)).astype(BF16)


def hartley_plane_pass(x, right, left):
    count, width = x.shape[0], x.shape[2]
    high, low = split(x.reshape(count * width, width))
    both = jnp.dot(jnp.concatenate([high, low], axis=1), right, preferred_element_type=F32)
    both = both[:, :width] + both[:, width:]
    planes = []
    for pair in range(count // 2):
        first = both[2 * pair * width : (2 * pair + 1) * width]
        second = both[(2 * pair + 1) * width : (2 * pair + 2) * width]
        high, low = split(jnp.concatenate([first, second], axis=1))
        result = jnp.dot(left, jnp.concatenate([high, low], axis=0), preferred_element_type=F32)
        result = result[:width] + result[width:]
        planes += [result[:, :width], result[:, width:]]
    return planes


def fold(x):
    return jnp.sum(x.reshape(-1, 8, x.shape[-1]), axis=0)


def kernel(
    ids_hbm,
    fiber_hbm,
    phase_ref,
    theta_ref,
    corner_ref,
    position_ref,
    choice_ref,
    right_ref,
    left_ref,
    modes_ref,
    out_ref,
    ids_ref,
    conduct_ref,
    spectrum_ref,
    line_ref,
    field_ref,
    moment_ref,
    info_ref,
    part_ref,
    stat_ref,
    load_sem,
    moment_send,
    moment_recv,
    info_send,
    info_recv,
    part_send,
    part_recv,
    stat_send,
    stat_recv,
):
    groups, slabs = lax.axis_size("macro"), lax.axis_size("pencil")
    macro, pencil = lax.axis_index("macro"), lax.axis_index("pencil")
    slab, width = conduct_ref.shape[0], conduct_ref.shape[2]
    owned = theta_ref.shape[0]
    volume = float(width) ** 3

    def loads(step):
        planes = pl.ds(step * GROUP, GROUP)
        return (
            pltpu.make_async_copy(ids_hbm.at[0, planes], ids_ref.at[planes], load_sem.at[0, step]),
            pltpu.make_async_copy(
                fiber_hbm.at[0, planes], conduct_ref.at[planes], load_sem.at[1, step]
            ),
        )

    for step in range(slab // GROUP):
        for load in loads(step):
            load.start()

    barrier = pltpu.get_barrier_semaphore()
    for k in range(1, slabs):
        pl.semaphore_signal(
            barrier, inc=1, device_id={"pencil": lax.rem(pencil + k, slabs)}, device_id_type=MESH
        )
    for k in range(1, groups):
        pl.semaphore_signal(
            barrier, inc=1, device_id={"macro": lax.rem(macro + k, groups)}, device_id_type=MESH
        )

    def ring(axis, here, size, source, target, send_sem, recv_sem):
        return [
            pltpu.make_async_remote_copy(
                src_ref=source,
                dst_ref=target(k),
                send_sem=send_sem.at[k],
                recv_sem=recv_sem.at[k],
                device_id={axis: lax.rem(here + k, size)},
                device_id_type=MESH,
            )
            for k in range(1, size)
        ]

    lane = lax.broadcasted_iota(jnp.int32, (1, 128), 1)
    hits = [jnp.where(lane == corner_ref[0, a], 1.0, 0.0) for a in range(8)]
    info = []
    for d in range(3):
        info.append(sum(hits[a] * (0.5 * (a >> d & 1) - 0.25) for a in range(8)))
    info.append(sum(hits) * 0.125)
    temperatures = jnp.zeros((1, 128), F32)
    rows = jnp.zeros((1, 128), F32)
    for n in range(owned):
        mine = lane == macro * owned + n
        temperatures = jnp.where(mine, theta_ref[n], temperatures)
        rows = jnp.where(mine, position_ref[n].astype(F32) + 1.0, rows)
    info += [temperatures, rows, jnp.zeros((1, 128), F32) + choice_ref[0].astype(F32)]
    info.append(jnp.zeros((1, 128), F32))
    info_ref[0] = jnp.concatenate(info, axis=0)

    def forward(step, carry):
        total, square = carry
        for load in loads(step):
            load.wait()
        planes = pl.ds(step * GROUP, GROUP)
        ids = ids_ref[planes]
        value = jnp.where(ids == 0, phase_ref[0, 0], phase_ref[0, PHASES - 1])
        for phase in range(1, PHASES - 1):
            value = jnp.where(ids == phase, phase_ref[0, phase], value)
        value = value * conduct_ref[planes]
        conduct_ref[planes] = value
        flat = value.reshape(GROUP * width, width)
        total = total + fold(flat)
        square = square + fold(flat * flat)
        scale = modes_ref[1]
        for i, plane in enumerate(hartley_plane_pass(value, right_ref[...], left_ref[...])):
            spectrum_ref[step * GROUP + i] = plane * scale
        return total, square

    zero = jnp.zeros((8, 128), F32)
    total, square = lax.fori_loop(0, slab // GROUP, forward, (zero, zero))

    def moments(block, carry):
        at = pl.ds(pl.multiple_of(block * BLOCK, BLOCK), BLOCK)
        root = modes_ref[0, at]
        power = jnp.ones_like(root)
        head = spectrum_ref[0, at]
        tail = head
        for x in range(1, slab):
            plane = spectrum_ref[x, at]
            power = power * root
            head = head + power * plane
            tail = plane + root * tail
        moment_ref[0, 0, at] = head
        moment_ref[0, 1, at] = tail
        return carry

    lax.fori_loop(0, width // BLOCK, moments, 0)

    pl.semaphore_wait(barrier, groups + slabs - 2)
    moment_copies = ring(
        "pencil", pencil, slabs, moment_ref.at[0], lambda k: moment_ref.at[k], moment_send, moment_recv
    )
    info_copies = ring(
        "macro", macro, groups, info_ref.at[0], lambda k: info_ref.at[k], info_send, info_recv
    )
    for copy in moment_copies + info_copies:
        copy.start()
    for copy in moment_copies:
        copy.wait()

    corner = sum(moment_ref[k, 0, :8, :] for k in range(slabs))
    first = (lax.broadcasted_iota(jnp.int32, (8, width), 0) == 0) & (
        lax.broadcasted_iota(jnp.int32, (8, width), 1) == 0
    )
    mean = jnp.sum(jnp.where(first, corner, 0.0))

    def solve(block, carry):
        at = pl.ds(pl.multiple_of(block * BLOCK, BLOCK), BLOCK)
        root, reach, closing = modes_ref[0, at], modes_ref[2, at], modes_ref[3, at]
        before = jnp.zeros_like(root)
        after = jnp.zeros_like(root)
        for i in range(slabs, 0, -1):
            before = before * reach + moment_ref[i % slabs, 1, at]
            after = after * reach + moment_ref[slabs - i, 0, at]
        before = before * closing
        after = after * closing
        back = after
        for x in range(slab - 1, -1, -1):
            back = root * back
            line_ref[x + 1, at] = back
            back = spectrum_ref[x, at] + back
        line_ref[0, at] = before + root * back
        ahead = before
        for x in range(slab):
            ahead = spectrum_ref[x, at] + root * ahead
            line_ref[x + 1, at] = line_ref[x + 1, at] + ahead
        line_ref[slab + 1, at] = root * ahead + after
        return carry

    lax.fori_loop(0, width // BLOCK, solve, 0)

    def place(x, plane):
        field_ref[x, PAD : PAD + width, :] = plane
        field_ref[x, PAD - 1 : PAD, :] = plane[width - 1 : width]
        field_ref[x, PAD + width : PAD + width + 1, :] = plane[:1]

    def backward(step, carry):
        planes = hartley_plane_pass(
            line_ref[pl.ds(1 + step * GROUP, GROUP)], right_ref[...], left_ref[...]
        )
        for i, plane in enumerate(planes):
            place(1 + step * GROUP + i, plane)
        return carry

    lax.fori_loop(0, slab // GROUP, backward, 0)
    edges = jnp.concatenate([line_ref[0:1], line_ref[slab + 1 : slab + 2]], axis=0)
    for x, plane in zip((0, slab + 1), hartley_plane_pass(edges, right_ref[...], left_ref[...])):
        place(x, plane)

    def lower(x):
        return pltpu.roll(x, 1, 1)

    def upper(x):
        return pltpu.roll(x, width - 1, 1)

    pairs = ((0, 0), (1, 1), (2, 2), (0, 1), (0, 2), (1, 2))

    def contract(x, sums):
        sums = list(sums)
        for block in range(width // BLOCK):

            def at(plane, shift):
                return field_ref[plane, PAD + block * BLOCK + shift : PAD + (block + 1) * BLOCK + shift, :]

            here, south, north = at(x + 1, 0), at(x + 1, -1), at(x + 1, 1)
            east, east_south = at(x + 2, 0), at(x + 2, -1)
            west, west_north = at(x, 0), at(x, 1)
            value = conduct_ref[x, block * BLOCK : (block + 1) * BLOCK, :]
            in_y, next_y = here - south, north - here
            out_x, into_x = east - here, here - west
            yy = next_y - in_y
            zz = (upper(here) - here) - (here - lower(here))
            second = [
                [mean - value - yy - zz, (east - east_south) - in_y, out_x - lower(out_x)],
                [next_y - (west_north - west), yy, next_y - lower(next_y)],
                [upper(into_x) - into_x, upper(in_y) - in_y, zz],
            ]
            weighted = [[value * second[e][d] for d in range(3)] for e in range(3)]
            for i, (d, f) in enumerate(pairs):
                product = sum(weighted[e][d] * second[e][f] for e in range(3))
                sums[i] = sums[i] + fold(product)
                sums[6 + i] = sums[6 + i] + fold(weighted[f][d])
        return tuple(sums)

    sums = lax.fori_loop(0, slab, contract, (zero,) * 12)
    tiles = [total, square, *sums, zero, zero]
    part_ref[pencil] = jnp.concatenate(
        [jnp.sum(tile, axis=0, keepdims=True) for tile in tiles], axis=0
    )
    part_copies = ring(
        "pencil", pencil, slabs, part_ref.at[pencil], lambda k: part_ref.at[pencil], part_send, part_recv
    )
    for copy in part_copies:
        copy.start()
    for copy in info_copies:
        copy.wait()
    theta = sum(info_ref[k, 4:5, :] for k in range(groups))
    target = sum(info_ref[k, 5:6, :] for k in range(groups))
    for copy in part_copies:
        copy.wait_send()
    for k in range(1, slabs):
        origin = lax.rem(pencil - k + slabs, slabs)
        pltpu.make_async_remote_copy(
            src_ref=part_ref.at[pencil],
            dst_ref=part_ref.at[origin],
            send_sem=part_send.at[k],
            recv_sem=part_recv.at[k],
            device_id={"pencil": origin},
            device_id_type=MESH,
        ).wait_recv()
    whole = sum(part_ref[s] for s in range(slabs))
    stat_ref[0] = jnp.zeros((STATS, 128), F32) + jnp.sum(whole, axis=1, keepdims=True)
    stat_copies = ring(
        "macro", macro, groups, stat_ref.at[0], lambda k: stat_ref.at[k], stat_send, stat_recv
    )
    for copy in stat_copies:
        copy.start()
    for copy in stat_copies:
        copy.wait()

    owners = [lax.rem(macro - k + groups, groups).astype(F32) for k in range(groups)]
    nodes = jnp.zeros((1, 128), F32)
    for q in range(groups):
        weights = info_ref[q]
        local = jnp.zeros((8, 128), F32) + jnp.sum(weights * theta, axis=1, keepdims=True)
        gradient = [local[d : d + 1] for d in range(3)]
        radiative = local[3:4] * local[3:4] * local[3:4]
        choice = weights[6:7]
        stats = jnp.zeros((STATS, 128), F32)
        for k in range(groups):
            stats = stats + jnp.where(choice == owners[k], stat_ref[k], 0.0)
        stats = stats * (1.0 / volume)
        average = stats[0:1]
        square_mean = stats[1:2] + 2.0 * radiative * average + radiative * radiative
        reference_k = jnp.sqrt(square_mean)
        factor = radiative - 2.0 * reference_k
        response = {}
        for i, (d, f) in enumerate(pairs):
            value = (stats[2 + i : 3 + i] - factor * stats[8 + i : 9 + i]) / square_mean
            response[d, f] = response[f, d] = value
        for d in range(3):
            flux = (average + radiative) * gradient[d]
            flux = flux + sum(response[d, e] * gradient[e] for e in range(3))
            nodes = nodes + flux * weights[d : d + 1]
            if q == 0:
                out_ref[d : d + 1, :] = flux
    for n in range(owned):
        wanted = (macro * owned + n + 1).astype(F32)
        row = jnp.sum(jnp.where(target == wanted, nodes, 0.0), axis=1, keepdims=True)
        out_ref[3 + n : 4 + n, :] = jnp.zeros((1, 128), F32) + row


def on_device(right, left, modes, groups, slabs, ids, fiber, phases, theta, corners, positions, choices):
    slab, width = fiber.shape[1], fiber.shape[3]
    owned = theta.shape[0]
    assert corners.shape[0] == 1 and groups * owned <= 128
    rows = -(-(3 + owned) // 8) * 8
    smem = pl.BlockSpec(memory_space=pltpu.SMEM)
    vmem = pl.BlockSpec(memory_space=pltpu.VMEM)
    whole = pl.BlockSpec(memory_space=pl.ANY)
    dma = pltpu.SemaphoreType.DMA
    out = pl.pallas_call(
        kernel,
        out_shape=jax.ShapeDtypeStruct((rows, 128), F32),
        in_specs=[whole, whole, smem, smem, smem, smem, smem, vmem, vmem, vmem],
        out_specs=vmem,
        scratch_shapes=[
            pltpu.VMEM((slab, width, width), jnp.int32),
            pltpu.VMEM((slab, width, width), F32),
            pltpu.VMEM((slab, width, width), F32),
            pltpu.VMEM((slab + 2, width, width), F32),
            pltpu.VMEM((slab + 2, width + 2 * PAD, width), F32),
            pltpu.VMEM((slabs, 2, width, width), F32),
            pltpu.VMEM((groups, 8, 128), F32),
            pltpu.VMEM((slabs, STATS, 128), F32),
            pltpu.VMEM((groups, STATS, 128), F32),
            dma((2, slab // GROUP)),
            dma((slabs,)),
            dma((slabs,)),
            dma((groups,)),
            dma((groups,)),
            dma((slabs,)),
            dma((slabs,)),
            dma((groups,)),
            dma((groups,)),
        ],
        compiler_params=pltpu.CompilerParams(
            collective_id=0, has_side_effects=True, vmem_limit_bytes=48 << 20
        ),
    )(ids, fiber, phases, theta, corners, positions, choices, right, left, modes)
    return out[:3, 0].reshape(1, 3), out[3 : 3 + owned, 0]


def solution(mesh):
    groups, slabs = mesh.shape["macro"], mesh.shape["pencil"]
    in_specs = (
        P("macro", "pencil", None, None),
        P("macro", "pencil", None, None),
        P("macro", None),
        P("macro"),
        P("macro", None),
        P("macro"),
        P("macro"),
    )
    out_specs = (P("macro", None), P("macro"))

    def run(ids, fiber, *rest):
        width = fiber.shape[3]
        right, left = hartley_tables(width)
        modes = mode_tables(width, fiber.shape[1] // slabs)
        body = functools.partial(
            on_device, jnp.asarray(right), jnp.asarray(left), jnp.asarray(modes), groups, slabs
        )
        return jax.shard_map(
            body, mesh=mesh, in_specs=in_specs, out_specs=out_specs, check_vma=False
        )(ids, fiber, *rest)

    return run
```

```python
import functools
import math

import jax
import jax.numpy as jnp
import numpy as np
from jax import lax
from jax.experimental import pallas as pl
from jax.experimental.pallas import tpu as pltpu
from jax.sharding import PartitionSpec as P

PHASES = 3
MESH = pl.DeviceIdType.MESH
F32 = jnp.float32
BF16 = jnp.bfloat16
GROUP = 4
STATS = 16
PAD = 8
BLOCK = 32


def hartley_tables(width):
    index = np.arange(width)
    angle = 2.0 * math.pi / width * (index[:, None] * index[None, :] % width)
    table = np.cos(angle) + np.sin(angle)
    high = table.astype(BF16)
    low = (table - high.astype(np.float64)).astype(BF16)
    right = np.concatenate([np.concatenate([high, low], axis=1)] * 2, axis=0)
    return right, np.ascontiguousarray(right.T)


def mode_tables(width, slab):
    line = 4.0 * np.sin(math.pi * np.arange(width) / width) ** 2
    lam = line[:, None] + line[None, :]
    safe = np.where(lam > 0, lam, 1.0)
    half = 1.0 + safe / 2.0
    root = half - np.sqrt(half * half - 1.0)
    scale = 1.0 / (1.0 / root - root) / width**2
    root[0, 0] = 1.0
    scale[0, 0] = 1.0 / width**3
    closing = 1.0 / (1.0 - np.where(lam > 0, root**width, 0.0))
    closing[0, 0] = 0.0
    return np.stack([root, scale, root**slab, closing]).astype(np.float32)


def split(x):
    high = x.astype(BF16)
    return high, (x - high.astype(F32)).astype(BF16)


def hartley_plane_pass(x, right, left):
    count, width = x.shape[0], x.shape[2]
    high, low = split(x.reshape(count * width, width))
    both = jnp.dot(jnp.concatenate([high, low], axis=1), right, preferred_element_type=F32)
    both = both[:, :width] + both[:, width:]
    planes = []
    for pair in range(count // 2):
        first = both[2 * pair * width : (2 * pair + 1) * width]
        second = both[(2 * pair + 1) * width : (2 * pair + 2) * width]
        high, low = split(jnp.concatenate([first, second], axis=1))
        result = jnp.dot(left, jnp.concatenate([high, low], axis=0), preferred_element_type=F32)
        result = result[:width] + result[width:]
        planes += [result[:, :width], result[:, width:]]
    return planes


def fold(x):
    return jnp.sum(x.reshape(-1, 8, x.shape[-1]), axis=0)


def kernel(
    ids_hbm,
    fiber_hbm,
    phase_hbm,
    theta_hbm,
    corner_hbm,
    position_hbm,
    choice_hbm,
    right_hbm,
    left_hbm,
    modes_hbm,
    out_ref,
    phase_ref,
    theta_ref,
    corner_ref,
    position_ref,
    choice_ref,
    right_ref,
    left_ref,
    modes_ref,
    ids_ref,
    conduct_ref,
    spectrum_ref,
    line_ref,
    field_ref,
    moment_ref,
    info_ref,
    part_ref,
    stat_ref,
    small_sem,
    load_sem,
    moment_send,
    moment_recv,
    info_send,
    info_recv,
    part_send,
    part_recv,
    stat_send,
    stat_recv,
):
    groups, slabs = lax.axis_size("macro"), lax.axis_size("pencil")
    macro, pencil = lax.axis_index("macro"), lax.axis_index("pencil")
    slab, width = conduct_ref.shape[0], conduct_ref.shape[2]
    owned = theta_ref.shape[0]
    volume = float(width) ** 3

    def loads(step):
        planes = pl.ds(step * GROUP, GROUP)
        return (
            pltpu.make_async_copy(ids_hbm.at[0, planes], ids_ref.at[planes], load_sem.at[0, step]),
            pltpu.make_async_copy(
                fiber_hbm.at[0, planes], conduct_ref.at[planes], load_sem.at[1, step]
            ),
        )

    small = [
        pltpu.make_async_copy(source, target, small_sem.at[i])
        for i, (source, target) in enumerate(
            (
                (phase_hbm, phase_ref),
                (right_hbm, right_ref),
                (left_hbm, left_ref),
                (modes_hbm, modes_ref),
                (theta_hbm, theta_ref),
                (corner_hbm, corner_ref),
                (position_hbm, position_ref),
                (choice_hbm, choice_ref),
            )
        )
    ]
    for copy in small[:3] + list(loads(0)) + small[3:]:
        copy.start()
    for step in range(1, slab // GROUP):
        for load in loads(step):
            load.start()

    barrier = pltpu.get_barrier_semaphore()
    for k in range(1, slabs):
        pl.semaphore_signal(
            barrier, inc=1, device_id={"pencil": lax.rem(pencil + k, slabs)}, device_id_type=MESH
        )
    for k in range(1, groups):
        pl.semaphore_signal(
            barrier, inc=1, device_id={"macro": lax.rem(macro + k, groups)}, device_id_type=MESH
        )

    def ring(axis, here, size, source, target, send_sem, recv_sem):
        return [
            pltpu.make_async_remote_copy(
                src_ref=source,
                dst_ref=target(k),
                send_sem=send_sem.at[k],
                recv_sem=recv_sem.at[k],
                device_id={axis: lax.rem(here + k, size)},
                device_id_type=MESH,
            )
            for k in range(1, size)
        ]

    for copy in small:
        copy.wait()
    lane = lax.broadcasted_iota(jnp.int32, (1, 128), 1)
    hits = [jnp.where(lane == corner_ref[0, a], 1.0, 0.0) for a in range(8)]
    info = []
    for d in range(3):
        info.append(sum(hits[a] * (0.5 * (a >> d & 1) - 0.25) for a in range(8)))
    info.append(sum(hits) * 0.125)
    temperatures = jnp.zeros((1, 128), F32)
    rows = jnp.zeros((1, 128), F32)
    for n in range(owned):
        mine = lane == macro * owned + n
        temperatures = jnp.where(mine, theta_ref[n], temperatures)
        rows = jnp.where(mine, position_ref[n].astype(F32) + 1.0, rows)
    info += [temperatures, rows, jnp.zeros((1, 128), F32) + choice_ref[0].astype(F32)]
    info.append(jnp.zeros((1, 128), F32))
    info_ref[0] = jnp.concatenate(info, axis=0)

    def forward(step, carry):
        total, square = carry
        for load in loads(step):
            load.wait()
        planes = pl.ds(step * GROUP, GROUP)
        ids = ids_ref[planes]
        value = jnp.where(ids == 0, phase_ref[0, 0], phase_ref[0, PHASES - 1])
        for phase in range(1, PHASES - 1):
            value = jnp.where(ids == phase, phase_ref[0, phase], value)
        value = value * conduct_ref[planes]
        conduct_ref[planes] = value
        flat = value.reshape(GROUP * width, width)
        total = total + fold(flat)
        square = square + fold(flat * flat)
        scale = modes_ref[1]
        for i, plane in enumerate(hartley_plane_pass(value, right_ref[...], left_ref[...])):
            spectrum_ref[step * GROUP + i] = plane * scale
        return total, square

    zero = jnp.zeros((8, 128), F32)
    total, square = lax.fori_loop(0, slab // GROUP, forward, (zero, zero))

    def moments(block, carry):
        at = pl.ds(pl.multiple_of(block * BLOCK, BLOCK), BLOCK)
        root = modes_ref[0, at]
        power = jnp.ones_like(root)
        head = spectrum_ref[0, at]
        tail = head
        for x in range(1, slab):
            plane = spectrum_ref[x, at]
            power = power * root
            head = head + power * plane
            tail = plane + root * tail
        moment_ref[0, 0, at] = head
        moment_ref[0, 1, at] = tail
        return carry

    lax.fori_loop(0, width // BLOCK, moments, 0)

    pl.semaphore_wait(barrier, groups + slabs - 2)
    moment_copies = ring(
        "pencil", pencil, slabs, moment_ref.at[0], lambda k: moment_ref.at[k], moment_send, moment_recv
    )
    info_copies = ring(
        "macro", macro, groups, info_ref.at[0], lambda k: info_ref.at[k], info_send, info_recv
    )
    for copy in moment_copies + info_copies:
        copy.start()
    for copy in moment_copies:
        copy.wait()

    corner = sum(moment_ref[k, 0, :8, :] for k in range(slabs))
    first = (lax.broadcasted_iota(jnp.int32, (8, width), 0) == 0) & (
        lax.broadcasted_iota(jnp.int32, (8, width), 1) == 0
    )
    mean = jnp.sum(jnp.where(first, corner, 0.0))

    def solve(block, carry):
        at = pl.ds(pl.multiple_of(block * BLOCK, BLOCK), BLOCK)
        root, reach, closing = modes_ref[0, at], modes_ref[2, at], modes_ref[3, at]
        before = jnp.zeros_like(root)
        after = jnp.zeros_like(root)
        for i in range(slabs, 0, -1):
            before = before * reach + moment_ref[i % slabs, 1, at]
            after = after * reach + moment_ref[slabs - i, 0, at]
        before = before * closing
        after = after * closing
        back = after
        for x in range(slab - 1, -1, -1):
            back = root * back
            line_ref[x + 1, at] = back
            back = spectrum_ref[x, at] + back
        line_ref[0, at] = before + root * back
        ahead = before
        for x in range(slab):
            ahead = spectrum_ref[x, at] + root * ahead
            line_ref[x + 1, at] = line_ref[x + 1, at] + ahead
        line_ref[slab + 1, at] = root * ahead + after
        return carry

    lax.fori_loop(0, width // BLOCK, solve, 0)

    def place(x, plane):
        field_ref[x, PAD : PAD + width, :] = plane
        field_ref[x, PAD - 1 : PAD, :] = plane[width - 1 : width]
        field_ref[x, PAD + width : PAD + width + 1, :] = plane[:1]

    def backward(step, carry):
        planes = hartley_plane_pass(
            line_ref[pl.ds(1 + step * GROUP, GROUP)], right_ref[...], left_ref[...]
        )
        for i, plane in enumerate(planes):
            place(1 + step * GROUP + i, plane)
        return carry

    lax.fori_loop(0, slab // GROUP, backward, 0)
    edges = jnp.concatenate([line_ref[0:1], line_ref[slab + 1 : slab + 2]], axis=0)
    for x, plane in zip((0, slab + 1), hartley_plane_pass(edges, right_ref[...], left_ref[...])):
        place(x, plane)

    def lower(x):
        return pltpu.roll(x, 1, 1)

    def upper(x):
        return pltpu.roll(x, width - 1, 1)

    pairs = ((0, 0), (1, 1), (2, 2), (0, 1), (0, 2), (1, 2))

    def contract(x, sums):
        sums = list(sums)
        for block in range(width // BLOCK):

            def at(plane, shift):
                return field_ref[plane, PAD + block * BLOCK + shift : PAD + (block + 1) * BLOCK + shift, :]

            here, south, north = at(x + 1, 0), at(x + 1, -1), at(x + 1, 1)
            east, east_south = at(x + 2, 0), at(x + 2, -1)
            west, west_north = at(x, 0), at(x, 1)
            value = conduct_ref[x, block * BLOCK : (block + 1) * BLOCK, :]
            in_y, next_y = here - south, north - here
            out_x, into_x = east - here, here - west
            yy = next_y - in_y
            zz = (upper(here) - here) - (here - lower(here))
            second = [
                [mean - value - yy - zz, (east - east_south) - in_y, out_x - lower(out_x)],
                [next_y - (west_north - west), yy, next_y - lower(next_y)],
                [upper(into_x) - into_x, upper(in_y) - in_y, zz],
            ]
            weighted = [[value * second[e][d] for d in range(3)] for e in range(3)]
            for i, (d, f) in enumerate(pairs):
                product = sum(weighted[e][d] * second[e][f] for e in range(3))
                sums[i] = sums[i] + fold(product)
                sums[6 + i] = sums[6 + i] + fold(weighted[f][d])
        return tuple(sums)

    sums = lax.fori_loop(0, slab, contract, (zero,) * 12)
    tiles = [total, square, *sums, zero, zero]
    part_ref[pencil] = jnp.concatenate(
        [jnp.sum(tile, axis=0, keepdims=True) for tile in tiles], axis=0
    )
    part_copies = ring(
        "pencil", pencil, slabs, part_ref.at[pencil], lambda k: part_ref.at[pencil], part_send, part_recv
    )
    for copy in part_copies:
        copy.start()
    for copy in info_copies:
        copy.wait()
    theta = sum(info_ref[k, 4:5, :] for k in range(groups))
    target = sum(info_ref[k, 5:6, :] for k in range(groups))
    for copy in part_copies:
        copy.wait_send()
    for k in range(1, slabs):
        origin = lax.rem(pencil - k + slabs, slabs)
        pltpu.make_async_remote_copy(
            src_ref=part_ref.at[pencil],
            dst_ref=part_ref.at[origin],
            send_sem=part_send.at[k],
            recv_sem=part_recv.at[k],
            device_id={"pencil": origin},
            device_id_type=MESH,
        ).wait_recv()
    whole = sum(part_ref[s] for s in range(slabs))
    stat_ref[0] = jnp.zeros((STATS, 128), F32) + jnp.sum(whole, axis=1, keepdims=True)
    stat_copies = ring(
        "macro", macro, groups, stat_ref.at[0], lambda k: stat_ref.at[k], stat_send, stat_recv
    )
    for copy in stat_copies:
        copy.start()
    for copy in stat_copies:
        copy.wait()

    owners = [lax.rem(macro - k + groups, groups).astype(F32) for k in range(groups)]
    nodes = jnp.zeros((1, 128), F32)
    for q in range(groups):
        weights = info_ref[q]
        local = jnp.zeros((8, 128), F32) + jnp.sum(weights * theta, axis=1, keepdims=True)
        gradient = [local[d : d + 1] for d in range(3)]
        radiative = local[3:4] * local[3:4] * local[3:4]
        choice = weights[6:7]
        stats = jnp.zeros((STATS, 128), F32)
        for k in range(groups):
            stats = stats + jnp.where(choice == owners[k], stat_ref[k], 0.0)
        stats = stats * (1.0 / volume)
        average = stats[0:1]
        square_mean = stats[1:2] + 2.0 * radiative * average + radiative * radiative
        reference_k = jnp.sqrt(square_mean)
        factor = radiative - 2.0 * reference_k
        response = {}
        for i, (d, f) in enumerate(pairs):
            value = (stats[2 + i : 3 + i] - factor * stats[8 + i : 9 + i]) / square_mean
            response[d, f] = response[f, d] = value
        for d in range(3):
            flux = (average + radiative) * gradient[d]
            flux = flux + sum(response[d, e] * gradient[e] for e in range(3))
            nodes = nodes + flux * weights[d : d + 1]
            if q == 0:
                out_ref[d : d + 1, :] = flux
    for n in range(owned):
        wanted = (macro * owned + n + 1).astype(F32)
        row = jnp.sum(jnp.where(target == wanted, nodes, 0.0), axis=1, keepdims=True)
        out_ref[3 + n : 4 + n, :] = jnp.zeros((1, 128), F32) + row


def on_device(right, left, modes, groups, slabs, ids, fiber, phases, theta, corners, positions, choices):
    slab, width = fiber.shape[1], fiber.shape[3]
    owned = theta.shape[0]
    assert corners.shape[0] == 1 and groups * owned <= 128
    rows = -(-(3 + owned) // 8) * 8
    vmem = pl.BlockSpec(memory_space=pltpu.VMEM)
    whole = pl.BlockSpec(memory_space=pltpu.HBM)
    dma = pltpu.SemaphoreType.DMA
    out = pl.pallas_call(
        kernel,
        out_shape=jax.ShapeDtypeStruct((rows, 128), F32),
        in_specs=[whole] * 10,
        out_specs=vmem,
        scratch_shapes=[
            pltpu.SMEM(phases.shape, F32),
            pltpu.SMEM(theta.shape, F32),
            pltpu.SMEM(corners.shape, jnp.int32),
            pltpu.SMEM(positions.shape, jnp.int32),
            pltpu.SMEM(choices.shape, jnp.int32),
            pltpu.VMEM(right.shape, BF16),
            pltpu.VMEM(left.shape, BF16),
            pltpu.VMEM(modes.shape, F32),
            pltpu.VMEM((slab, width, width), jnp.int32),
            pltpu.VMEM((slab, width, width), F32),
            pltpu.VMEM((slab, width, width), F32),
            pltpu.VMEM((slab + 2, width, width), F32),
            pltpu.VMEM((slab + 2, width + 2 * PAD, width), F32),
            pltpu.VMEM((slabs, 2, width, width), F32),
            pltpu.VMEM((groups, 8, 128), F32),
            pltpu.VMEM((slabs, STATS, 128), F32),
            pltpu.VMEM((groups, STATS, 128), F32),
            dma((8,)),
            dma((2, slab // GROUP)),
            dma((slabs,)),
            dma((slabs,)),
            dma((groups,)),
            dma((groups,)),
            dma((slabs,)),
            dma((slabs,)),
            dma((groups,)),
            dma((groups,)),
        ],
        compiler_params=pltpu.CompilerParams(
            collective_id=0, has_side_effects=True, vmem_limit_bytes=60 << 20
        ),
    )(ids, fiber, phases, theta, corners, positions, choices, right, left, modes)
    return out[:3, 0].reshape(1, 3), out[3 : 3 + owned, 0]


def solution(mesh):
    groups, slabs = mesh.shape["macro"], mesh.shape["pencil"]
    in_specs = (
        P("macro", "pencil", None, None),
        P("macro", "pencil", None, None),
        P("macro", None),
        P("macro"),
        P("macro", None),
        P("macro"),
        P("macro"),
    )
    out_specs = (P("macro", None), P("macro"))

    def run(ids, fiber, *rest):
        width = fiber.shape[3]
        right, left = hartley_tables(width)
        modes = mode_tables(width, fiber.shape[1] // slabs)
        body = functools.partial(
            on_device, jnp.asarray(right), jnp.asarray(left), jnp.asarray(modes), groups, slabs
        )
        return jax.shard_map(
            body, mesh=mesh, in_specs=in_specs, out_specs=out_specs, check_vma=False
        )(ids, fiber, *rest)

    return run
```

```python
import functools
import math

import jax
import jax.numpy as jnp
import numpy as np
from jax import lax
from jax.experimental import pallas as pl
from jax.experimental.pallas import tpu as pltpu
from jax.sharding import PartitionSpec as P

PHASES = 3
MESH = pl.DeviceIdType.MESH
F32 = jnp.float32
BF16 = jnp.bfloat16
GROUP = 4
STATS = 16
PAD = 8
BLOCK = 32
ROWS = 8


def hartley_tables(width):
    index = np.arange(width)
    angle = 2.0 * math.pi / width * (index[:, None] * index[None, :] % width)
    table = np.cos(angle) + np.sin(angle)
    high = table.astype(BF16)
    low = (table - high.astype(np.float64)).astype(BF16)
    right = np.concatenate([np.concatenate([high, low], axis=1)] * 2, axis=0)
    return right, np.ascontiguousarray(right.T)


def mode_tables(width, slab):
    line = 4.0 * np.sin(math.pi * np.arange(width) / width) ** 2
    lam = line[:, None] + line[None, :]
    safe = np.where(lam > 0, lam, 1.0)
    half = 1.0 + safe / 2.0
    root = half - np.sqrt(half * half - 1.0)
    scale = 1.0 / (1.0 / root - root) / width**2
    root[0, 0] = 1.0
    scale[0, 0] = 1.0 / width**3
    closing = 1.0 / (1.0 - np.where(lam > 0, root**width, 0.0))
    closing[0, 0] = 0.0
    return np.stack([root, scale, root**slab, closing]).astype(np.float32)


def split(x):
    high = x.astype(BF16)
    return high, (x - high.astype(F32)).astype(BF16)


def hartley_plane_pass(x, right, left):
    count, width = x.shape[0], x.shape[2]
    high, low = split(x.reshape(count * width, width))
    both = jnp.dot(jnp.concatenate([high, low], axis=1), right, preferred_element_type=F32)
    both = both[:, :width] + both[:, width:]
    planes = []
    for pair in range(count // 2):
        first = both[2 * pair * width : (2 * pair + 1) * width]
        second = both[(2 * pair + 1) * width : (2 * pair + 2) * width]
        high, low = split(jnp.concatenate([first, second], axis=1))
        result = jnp.dot(left, jnp.concatenate([high, low], axis=0), preferred_element_type=F32)
        result = result[:width] + result[width:]
        planes += [result[:, :width], result[:, width:]]
    return planes


def forward_plane_pass(x, right, left):
    count, width = x.shape[0], x.shape[2]
    flat = x.reshape(count * width, width).astype(BF16)
    both = jnp.dot(flat, right[:width], preferred_element_type=F32)
    both = (both[:, :width] + both[:, width:]).astype(BF16)
    planes = []
    for pair in range(count // 2):
        first = both[2 * pair * width : (2 * pair + 1) * width]
        second = both[(2 * pair + 1) * width : (2 * pair + 2) * width]
        data = jnp.concatenate([first, second], axis=1)
        result = jnp.dot(left[:, :width], data, preferred_element_type=F32)
        result = result[:width] + result[width:]
        planes += [result[:, :width], result[:, width:]]
    return planes


def fold(x):
    return jnp.sum(x.reshape(-1, 8, x.shape[-1]), axis=0)


def kernel(
    ids_hbm,
    fiber_hbm,
    phase_hbm,
    theta_hbm,
    corner_hbm,
    position_hbm,
    choice_hbm,
    right_hbm,
    left_hbm,
    modes_hbm,
    out_ref,
    phase_ref,
    theta_ref,
    corner_ref,
    position_ref,
    choice_ref,
    right_ref,
    left_ref,
    modes_ref,
    ids_ref,
    conduct_ref,
    spectrum_ref,
    line_ref,
    field_ref,
    moment_ref,
    info_ref,
    part_ref,
    stat_ref,
    small_sem,
    load_sem,
    moment_send,
    moment_recv,
    info_send,
    info_recv,
    part_send,
    part_recv,
    stat_send,
    stat_recv,
):
    groups, slabs = lax.axis_size("macro"), lax.axis_size("pencil")
    macro, pencil = lax.axis_index("macro"), lax.axis_index("pencil")
    slab, width = conduct_ref.shape[0], conduct_ref.shape[2]
    owned = theta_ref.shape[0]
    volume = float(width) ** 3

    def loads(step):
        planes = pl.ds(step * GROUP, GROUP)
        return (
            pltpu.make_async_copy(ids_hbm.at[0, planes], ids_ref.at[planes], load_sem.at[0, step]),
            pltpu.make_async_copy(
                fiber_hbm.at[0, planes], conduct_ref.at[planes], load_sem.at[1, step]
            ),
        )

    small = [
        pltpu.make_async_copy(source, target, small_sem.at[i])
        for i, (source, target) in enumerate(
            (
                (phase_hbm, phase_ref),
                (right_hbm, right_ref),
                (left_hbm, left_ref),
                (modes_hbm, modes_ref),
                (theta_hbm, theta_ref),
                (corner_hbm, corner_ref),
                (position_hbm, position_ref),
                (choice_hbm, choice_ref),
            )
        )
    ]
    for copy in small[:3] + list(loads(0)) + small[3:]:
        copy.start()
    for step in range(1, slab // GROUP):
        for load in loads(step):
            load.start()

    barrier = pltpu.get_barrier_semaphore()
    for k in range(1, slabs):
        pl.semaphore_signal(
            barrier, inc=1, device_id={"pencil": lax.rem(pencil + k, slabs)}, device_id_type=MESH
        )
    for k in range(1, groups):
        pl.semaphore_signal(
            barrier, inc=1, device_id={"macro": lax.rem(macro + k, groups)}, device_id_type=MESH
        )

    def ring(axis, here, size, source, target, send_sem, recv_sem):
        return [
            pltpu.make_async_remote_copy(
                src_ref=source,
                dst_ref=target(k),
                send_sem=send_sem.at[k],
                recv_sem=recv_sem.at[k],
                device_id={axis: lax.rem(here + k, size)},
                device_id_type=MESH,
            )
            for k in range(1, size)
        ]

    for copy in small:
        copy.wait()
    lane = lax.broadcasted_iota(jnp.int32, (1, 128), 1)
    hits = [jnp.where(lane == corner_ref[0, a], 1.0, 0.0) for a in range(8)]
    info = []
    for d in range(3):
        info.append(sum(hits[a] * (0.5 * (a >> d & 1) - 0.25) for a in range(8)))
    info.append(sum(hits) * 0.125)
    temperatures = jnp.zeros((1, 128), F32)
    rows = jnp.zeros((1, 128), F32)
    for n in range(owned):
        mine = lane == macro * owned + n
        temperatures = jnp.where(mine, theta_ref[n], temperatures)
        rows = jnp.where(mine, position_ref[n].astype(F32) + 1.0, rows)
    info += [temperatures, rows, jnp.zeros((1, 128), F32) + choice_ref[0].astype(F32)]
    info.append(jnp.zeros((1, 128), F32))
    info_ref[0] = jnp.concatenate(info, axis=0)

    def forward(step, carry):
        total, square = carry
        for load in loads(step):
            load.wait()
        planes = pl.ds(step * GROUP, GROUP)
        ids = ids_ref[planes]
        value = jnp.where(ids == 0, phase_ref[0, 0], phase_ref[0, PHASES - 1])
        for phase in range(1, PHASES - 1):
            value = jnp.where(ids == phase, phase_ref[0, phase], value)
        value = value * conduct_ref[planes]
        conduct_ref[planes] = value
        flat = value.reshape(GROUP * width, width)
        total = total + fold(flat)
        square = square + fold(flat * flat)
        scale = modes_ref[1]
        for i, plane in enumerate(forward_plane_pass(value, right_ref[...], left_ref[...])):
            spectrum_ref[step * GROUP + i] = plane * scale
        return total, square

    zero = jnp.zeros((8, 128), F32)
    total, square = lax.fori_loop(0, slab // GROUP, forward, (zero, zero))

    def moments(block, carry):
        at = pl.ds(pl.multiple_of(block * BLOCK, BLOCK), BLOCK)
        root = modes_ref[0, at]
        power = jnp.ones_like(root)
        head = spectrum_ref[0, at]
        tail = head
        for x in range(1, slab):
            plane = spectrum_ref[x, at]
            power = power * root
            head = head + power * plane
            tail = plane + root * tail
        moment_ref[0, 0, at] = head
        moment_ref[0, 1, at] = tail
        return carry

    lax.fori_loop(0, width // BLOCK, moments, 0)
    first = (lax.broadcasted_iota(jnp.int32, (8, width), 0) == 0) & (
        lax.broadcasted_iota(jnp.int32, (8, width), 1) == 0
    )
    moment_ref[0, 0, :8] = jnp.where(first, jnp.sum(total) * (1.0 / volume), moment_ref[0, 0, :8])

    pl.semaphore_wait(barrier, groups + slabs - 2)
    moment_copies = ring(
        "pencil", pencil, slabs, moment_ref.at[0], lambda k: moment_ref.at[k], moment_send, moment_recv
    )
    info_copies = ring(
        "macro", macro, groups, info_ref.at[0], lambda k: info_ref.at[k], info_send, info_recv
    )
    for copy in moment_copies + info_copies:
        copy.start()
    for copy in moment_copies:
        copy.wait()

    corner = sum(moment_ref[k, 0, :8, :] for k in range(slabs))
    mean = jnp.sum(jnp.where(first, corner, 0.0))

    def solve(block, carry):
        at = pl.ds(pl.multiple_of(block * BLOCK, BLOCK), BLOCK)
        root, reach, closing = modes_ref[0, at], modes_ref[2, at], modes_ref[3, at]
        before = jnp.zeros_like(root)
        after = jnp.zeros_like(root)
        for i in range(slabs, 0, -1):
            before = before * reach + moment_ref[i % slabs, 1, at]
            after = after * reach + moment_ref[slabs - i, 0, at]
        before = before * closing
        after = after * closing
        back = after
        for x in range(slab - 1, -1, -1):
            back = root * back
            line_ref[x + 1, at] = back
            back = spectrum_ref[x, at] + back
        line_ref[0, at] = before + root * back
        ahead = before
        for x in range(slab):
            ahead = spectrum_ref[x, at] + root * ahead
            line_ref[x + 1, at] = line_ref[x + 1, at] + ahead
        line_ref[slab + 1, at] = root * ahead + after
        return carry

    lax.fori_loop(0, width // BLOCK, solve, 0)

    def place(x, plane):
        field_ref[x, PAD : PAD + width, :] = plane
        field_ref[x, PAD - 1 : PAD, :] = plane[width - 1 : width]
        field_ref[x, PAD + width : PAD + width + 1, :] = plane[:1]

    def backward(step, carry):
        planes = hartley_plane_pass(
            line_ref[pl.ds(1 + step * GROUP, GROUP)], right_ref[...], left_ref[...]
        )
        for i, plane in enumerate(planes):
            place(1 + step * GROUP + i, plane)
        return carry

    lax.fori_loop(0, slab // GROUP, backward, 0)
    edges = jnp.concatenate([line_ref[0:1], line_ref[slab + 1 : slab + 2]], axis=0)
    for x, plane in zip((0, slab + 1), hartley_plane_pass(edges, right_ref[...], left_ref[...])):
        place(x, plane)

    def lower(x):
        return pltpu.roll(x, 1, 1)

    def upper(x):
        return pltpu.roll(x, width - 1, 1)

    pairs = ((0, 0), (1, 1), (2, 2), (0, 1), (0, 2), (1, 2))

    def contract(x, sums):
        sums = list(sums)
        for block in range(width // ROWS):

            def at(plane, shift):
                return field_ref[plane, PAD + block * ROWS + shift : PAD + (block + 1) * ROWS + shift, :]

            here, south, north = at(x + 1, 0), at(x + 1, -1), at(x + 1, 1)
            east, east_south = at(x + 2, 0), at(x + 2, -1)
            west, west_north = at(x, 0), at(x, 1)
            value = conduct_ref[x, block * ROWS : (block + 1) * ROWS, :]
            in_y, next_y = here - south, north - here
            out_x, into_x = east - here, here - west
            yy = next_y - in_y
            zz = (upper(here) - here) - (here - lower(here))
            second = [
                [mean - value - yy - zz, (east - east_south) - in_y, out_x - lower(out_x)],
                [next_y - (west_north - west), yy, next_y - lower(next_y)],
                [upper(into_x) - into_x, upper(in_y) - in_y, zz],
            ]
            weighted = [[value * second[e][d] for d in range(3)] for e in range(3)]
            for i, (d, f) in enumerate(pairs):
                product = sum(weighted[e][d] * second[e][f] for e in range(3))
                sums[i] = sums[i] + fold(product)
                sums[6 + i] = sums[6 + i] + fold(weighted[f][d])
        return tuple(sums)

    sums = lax.fori_loop(0, slab, contract, (zero,) * 12)
    tiles = [total, square, *sums, zero, zero]
    part_ref[pencil] = jnp.concatenate(
        [jnp.sum(tile, axis=0, keepdims=True) for tile in tiles], axis=0
    )
    part_copies = ring(
        "pencil", pencil, slabs, part_ref.at[pencil], lambda k: part_ref.at[pencil], part_send, part_recv
    )
    for copy in part_copies:
        copy.start()
    for copy in info_copies:
        copy.wait()
    theta = sum(info_ref[k, 4:5, :] for k in range(groups))
    target = sum(info_ref[k, 5:6, :] for k in range(groups))
    for copy in part_copies:
        copy.wait_send()
    for k in range(1, slabs):
        origin = lax.rem(pencil - k + slabs, slabs)
        pltpu.make_async_remote_copy(
            src_ref=part_ref.at[pencil],
            dst_ref=part_ref.at[origin],
            send_sem=part_send.at[k],
            recv_sem=part_recv.at[k],
            device_id={"pencil": origin},
            device_id_type=MESH,
        ).wait_recv()
    whole = sum(part_ref[s] for s in range(slabs))
    stat_ref[0] = jnp.zeros((STATS, 128), F32) + jnp.sum(whole, axis=1, keepdims=True)
    stat_copies = ring(
        "macro", macro, groups, stat_ref.at[0], lambda k: stat_ref.at[k], stat_send, stat_recv
    )
    for copy in stat_copies:
        copy.start()
    for copy in stat_copies:
        copy.wait()

    owners = [lax.rem(macro - k + groups, groups).astype(F32) for k in range(groups)]
    nodes = jnp.zeros((1, 128), F32)
    for q in range(groups):
        weights = info_ref[q]
        local = jnp.zeros((8, 128), F32) + jnp.sum(weights * theta, axis=1, keepdims=True)
        gradient = [local[d : d + 1] for d in range(3)]
        radiative = local[3:4] * local[3:4] * local[3:4]
        choice = weights[6:7]
        stats = jnp.zeros((STATS, 128), F32)
        for k in range(groups):
            stats = stats + jnp.where(choice == owners[k], stat_ref[k], 0.0)
        stats = stats * (1.0 / volume)
        average = stats[0:1]
        square_mean = stats[1:2] + 2.0 * radiative * average + radiative * radiative
        reference_k = jnp.sqrt(square_mean)
        factor = radiative - 2.0 * reference_k
        response = {}
        for i, (d, f) in enumerate(pairs):
            value = (stats[2 + i : 3 + i] - factor * stats[8 + i : 9 + i]) / square_mean
            response[d, f] = response[f, d] = value
        for d in range(3):
            flux = (average + radiative) * gradient[d]
            flux = flux + sum(response[d, e] * gradient[e] for e in range(3))
            nodes = nodes + flux * weights[d : d + 1]
            if q == 0:
                out_ref[d : d + 1, :] = flux
    for n in range(owned):
        wanted = (macro * owned + n + 1).astype(F32)
        row = jnp.sum(jnp.where(target == wanted, nodes, 0.0), axis=1, keepdims=True)
        out_ref[3 + n : 4 + n, :] = jnp.zeros((1, 128), F32) + row


def on_device(right, left, modes, groups, slabs, ids, fiber, phases, theta, corners, positions, choices):
    slab, width = fiber.shape[1], fiber.shape[3]
    owned = theta.shape[0]
    assert corners.shape[0] == 1 and groups * owned <= 128
    rows = -(-(3 + owned) // 8) * 8
    vmem = pl.BlockSpec(memory_space=pltpu.VMEM)
    whole = pl.BlockSpec(memory_space=pltpu.HBM)
    dma = pltpu.SemaphoreType.DMA
    out = pl.pallas_call(
        kernel,
        out_shape=jax.ShapeDtypeStruct((rows, 128), F32),
        in_specs=[whole] * 10,
        out_specs=vmem,
        scratch_shapes=[
            pltpu.SMEM(phases.shape, F32),
            pltpu.SMEM(theta.shape, F32),
            pltpu.SMEM(corners.shape, jnp.int32),
            pltpu.SMEM(positions.shape, jnp.int32),
            pltpu.SMEM(choices.shape, jnp.int32),
            pltpu.VMEM(right.shape, BF16),
            pltpu.VMEM(left.shape, BF16),
            pltpu.VMEM(modes.shape, F32),
            pltpu.VMEM((slab, width, width), jnp.int32),
            pltpu.VMEM((slab, width, width), F32),
            pltpu.VMEM((slab, width, width), F32),
            pltpu.VMEM((slab + 2, width, width), F32),
            pltpu.VMEM((slab + 2, width + 2 * PAD, width), F32),
            pltpu.VMEM((slabs, 2, width, width), F32),
            pltpu.VMEM((groups, 8, 128), F32),
            pltpu.VMEM((slabs, STATS, 128), F32),
            pltpu.VMEM((groups, STATS, 128), F32),
            dma((8,)),
            dma((2, slab // GROUP)),
            dma((slabs,)),
            dma((slabs,)),
            dma((groups,)),
            dma((groups,)),
            dma((slabs,)),
            dma((slabs,)),
            dma((groups,)),
            dma((groups,)),
        ],
        compiler_params=pltpu.CompilerParams(
            collective_id=0, has_side_effects=True, vmem_limit_bytes=20 << 20
        ),
    )(ids, fiber, phases, theta, corners, positions, choices, right, left, modes)
    return out[:3, 0].reshape(1, 3), out[3 : 3 + owned, 0]


def solution(mesh):
    groups, slabs = mesh.shape["macro"], mesh.shape["pencil"]
    in_specs = (
        P("macro", "pencil", None, None),
        P("macro", "pencil", None, None),
        P("macro", None),
        P("macro"),
        P("macro", None),
        P("macro"),
        P("macro"),
    )
    out_specs = (P("macro", None), P("macro"))

    def run(ids, fiber, *rest):
        width = fiber.shape[3]
        right, left = hartley_tables(width)
        modes = mode_tables(width, fiber.shape[1] // slabs)
        body = functools.partial(
            on_device, jnp.asarray(right), jnp.asarray(left), jnp.asarray(modes), groups, slabs
        )
        return jax.shard_map(
            body, mesh=mesh, in_specs=in_specs, out_specs=out_specs, check_vma=False
        )(ids, fiber, *rest)

    return run
```

```python
import functools
import math

import jax
import jax.numpy as jnp
import numpy as np
from jax import lax
from jax.experimental import pallas as pl
from jax.experimental.pallas import tpu as pltpu
from jax.sharding import PartitionSpec as P

PHASES = 3
MESH = pl.DeviceIdType.MESH
F32 = jnp.float32
BF16 = jnp.bfloat16
GROUP = 4
STATS = 16
PAD = 8
BLOCK = 32
ROWS = 8


def hartley_tables(width):
    index = np.arange(width)
    angle = 2.0 * math.pi / width * (index[:, None] * index[None, :] % width)
    table = np.cos(angle) + np.sin(angle)
    high = table.astype(BF16)
    low = (table - high.astype(np.float64)).astype(BF16)
    right = np.concatenate([np.concatenate([high, low], axis=1)] * 2, axis=0)
    return right, np.ascontiguousarray(right.T)


def mode_tables(width, slab):
    line = 4.0 * np.sin(math.pi * np.arange(width) / width) ** 2
    lam = line[:, None] + line[None, :]
    safe = np.where(lam > 0, lam, 1.0)
    half = 1.0 + safe / 2.0
    root = half - np.sqrt(half * half - 1.0)
    scale = 1.0 / (1.0 / root - root) / width**2
    root[0, 0] = 1.0
    scale[0, 0] = 1.0 / width**3
    closing = 1.0 / (1.0 - np.where(lam > 0, root**width, 0.0))
    closing[0, 0] = 0.0
    return np.stack([root, scale, root**slab, closing]).astype(np.float32)


def split(x):
    high = x.astype(BF16)
    return high, (x - high.astype(F32)).astype(BF16)


def hartley_plane_pass(x, right, left):
    count, width = x.shape[0], x.shape[2]
    high, low = split(x.reshape(count * width, width))
    both = jnp.dot(jnp.concatenate([high, low], axis=1), right, preferred_element_type=F32)
    both = both[:, :width] + both[:, width:]
    planes = []
    for pair in range(count // 2):
        first = both[2 * pair * width : (2 * pair + 1) * width]
        second = both[(2 * pair + 1) * width : (2 * pair + 2) * width]
        high, low = split(jnp.concatenate([first, second], axis=1))
        result = jnp.dot(left, jnp.concatenate([high, low], axis=0), preferred_element_type=F32)
        result = result[:width] + result[width:]
        planes += [result[:, :width], result[:, width:]]
    return planes


def forward_plane_pass(x, right, left):
    count, width = x.shape[0], x.shape[2]
    flat = x.reshape(count * width, width).astype(BF16)
    both = jnp.dot(flat, right[:width], preferred_element_type=F32)
    both = (both[:, :width] + both[:, width:]).astype(BF16)
    planes = []
    for pair in range(count // 2):
        first = both[2 * pair * width : (2 * pair + 1) * width]
        second = both[(2 * pair + 1) * width : (2 * pair + 2) * width]
        data = jnp.concatenate([first, second], axis=1)
        result = jnp.dot(left[:, :width], data, preferred_element_type=F32)
        result = result[:width] + result[width:]
        planes += [result[:, :width], result[:, width:]]
    return planes


def fold(x):
    return jnp.sum(x.reshape(-1, 8, x.shape[-1]), axis=0)


def kernel(
    ids_hbm,
    fiber_hbm,
    phase_hbm,
    theta_hbm,
    corner_hbm,
    position_hbm,
    choice_hbm,
    right_hbm,
    left_hbm,
    modes_hbm,
    out_ref,
    phase_ref,
    theta_ref,
    corner_ref,
    position_ref,
    choice_ref,
    right_ref,
    left_ref,
    modes_ref,
    ids_ref,
    conduct_ref,
    spectrum_ref,
    line_ref,
    field_ref,
    moment_ref,
    info_ref,
    part_ref,
    stat_ref,
    small_sem,
    load_sem,
    moment_send,
    moment_recv,
    info_send,
    info_recv,
    part_send,
    part_recv,
    stat_send,
    stat_recv,
):
    groups, slabs = lax.axis_size("macro"), lax.axis_size("pencil")
    macro, pencil = lax.axis_index("macro"), lax.axis_index("pencil")
    slab, width = conduct_ref.shape[0], conduct_ref.shape[2]
    owned = theta_ref.shape[0]
    volume = float(width) ** 3

    def loads(step):
        planes = pl.ds(step * GROUP, GROUP)
        return (
            pltpu.make_async_copy(ids_hbm.at[0, planes], ids_ref.at[planes], load_sem.at[0, step]),
            pltpu.make_async_copy(
                fiber_hbm.at[0, planes], conduct_ref.at[planes], load_sem.at[1, step]
            ),
        )

    small = [
        pltpu.make_async_copy(source, target, small_sem.at[i])
        for i, (source, target) in enumerate(
            (
                (phase_hbm, phase_ref),
                (right_hbm, right_ref),
                (left_hbm, left_ref),
                (modes_hbm, modes_ref),
                (theta_hbm, theta_ref),
                (corner_hbm, corner_ref),
                (position_hbm, position_ref),
                (choice_hbm, choice_ref),
            )
        )
    ]
    for copy in small[:3] + list(loads(0)) + small[3:]:
        copy.start()
    for step in range(1, slab // GROUP):
        for load in loads(step):
            load.start()

    barrier = pltpu.get_barrier_semaphore()
    for k in range(1, slabs):
        pl.semaphore_signal(
            barrier, inc=1, device_id={"pencil": lax.rem(pencil + k, slabs)}, device_id_type=MESH
        )
    for k in range(1, groups):
        pl.semaphore_signal(
            barrier, inc=1, device_id={"macro": lax.rem(macro + k, groups)}, device_id_type=MESH
        )

    def ring(axis, here, size, source, target, send_sem, recv_sem):
        return [
            pltpu.make_async_remote_copy(
                src_ref=source,
                dst_ref=target(k),
                send_sem=send_sem.at[k],
                recv_sem=recv_sem.at[k],
                device_id={axis: lax.rem(here + k, size)},
                device_id_type=MESH,
            )
            for k in range(1, size)
        ]

    for copy in small:
        copy.wait()
    lane = lax.broadcasted_iota(jnp.int32, (1, 128), 1)
    hits = [jnp.where(lane == corner_ref[0, a], 1.0, 0.0) for a in range(8)]
    info = []
    for d in range(3):
        info.append(sum(hits[a] * (0.5 * (a >> d & 1) - 0.25) for a in range(8)))
    info.append(sum(hits) * 0.125)
    temperatures = jnp.zeros((1, 128), F32)
    rows = jnp.zeros((1, 128), F32)
    for n in range(owned):
        mine = lane == macro * owned + n
        temperatures = jnp.where(mine, theta_ref[n], temperatures)
        rows = jnp.where(mine, position_ref[n].astype(F32) + 1.0, rows)
    info += [temperatures, rows, jnp.zeros((1, 128), F32) + choice_ref[0].astype(F32)]
    info.append(jnp.zeros((1, 128), F32))
    info_ref[0] = jnp.concatenate(info, axis=0)

    def forward(step, carry):
        total, square = carry
        for load in loads(step):
            load.wait()
        planes = pl.ds(step * GROUP, GROUP)
        ids = ids_ref[planes]
        value = jnp.where(ids == 0, phase_ref[0, 0], phase_ref[0, PHASES - 1])
        for phase in range(1, PHASES - 1):
            value = jnp.where(ids == phase, phase_ref[0, phase], value)
        value = value * conduct_ref[planes]
        conduct_ref[planes] = value
        flat = value.reshape(GROUP * width, width)
        total = total + fold(flat)
        square = square + fold(flat * flat)
        scale = modes_ref[1]
        for i, plane in enumerate(forward_plane_pass(value, right_ref[...], left_ref[...])):
            spectrum_ref[step * GROUP + i] = plane * scale
        return total, square

    zero = jnp.zeros((8, 128), F32)
    total, square = lax.fori_loop(0, slab // GROUP, forward, (zero, zero))

    def moments(block, carry):
        at = pl.ds(pl.multiple_of(block * BLOCK, BLOCK), BLOCK)
        root = modes_ref[0, at]
        power = jnp.ones_like(root)
        head = spectrum_ref[0, at]
        tail = head
        for x in range(1, slab):
            plane = spectrum_ref[x, at]
            power = power * root
            head = head + power * plane
            tail = plane + root * tail
        moment_ref[0, 0, at] = head
        moment_ref[0, 1, at] = tail
        return carry

    lax.fori_loop(0, width // BLOCK, moments, 0)
    first = (lax.broadcasted_iota(jnp.int32, (8, width), 0) == 0) & (
        lax.broadcasted_iota(jnp.int32, (8, width), 1) == 0
    )
    moment_ref[0, 0, :8] = jnp.where(first, jnp.sum(total) * (1.0 / volume), moment_ref[0, 0, :8])

    pl.semaphore_wait(barrier, groups + slabs - 2)
    moment_copies = ring(
        "pencil", pencil, slabs, moment_ref.at[0], lambda k: moment_ref.at[k], moment_send, moment_recv
    )
    info_copies = ring(
        "macro", macro, groups, info_ref.at[0], lambda k: info_ref.at[k], info_send, info_recv
    )
    for copy in moment_copies + info_copies:
        copy.start()
    for copy in moment_copies:
        copy.wait()

    corner = sum(moment_ref[k, 0, :8, :] for k in range(slabs))
    mean = jnp.sum(jnp.where(first, corner, 0.0))

    def solve(block, carry):
        at = pl.ds(pl.multiple_of(block * BLOCK, BLOCK), BLOCK)
        root, reach, closing = modes_ref[0, at], modes_ref[2, at], modes_ref[3, at]
        before = jnp.zeros_like(root)
        after = jnp.zeros_like(root)
        for i in range(slabs, 0, -1):
            before = before * reach + moment_ref[i % slabs, 1, at]
            after = after * reach + moment_ref[slabs - i, 0, at]
        before = before * closing
        after = after * closing
        back = after
        for x in range(slab - 1, -1, -1):
            back = root * back
            line_ref[x + 1, at] = back
            back = spectrum_ref[x, at] + back
        line_ref[0, at] = before + root * back
        ahead = before
        for x in range(slab):
            ahead = spectrum_ref[x, at] + root * ahead
            line_ref[x + 1, at] = line_ref[x + 1, at] + ahead
        line_ref[slab + 1, at] = root * ahead + after
        return carry

    lax.fori_loop(0, width // BLOCK, solve, 0)

    def place(x, plane):
        field_ref[x, PAD : PAD + width, :] = plane
        field_ref[x, PAD - 1 : PAD, :] = plane[width - 1 : width]
        field_ref[x, PAD + width : PAD + width + 1, :] = plane[:1]

    def backward(step, carry):
        planes = hartley_plane_pass(
            line_ref[pl.ds(1 + step * GROUP, GROUP)], right_ref[...], left_ref[...]
        )
        for i, plane in enumerate(planes):
            place(1 + step * GROUP + i, plane)
        return carry

    lax.fori_loop(0, slab // GROUP, backward, 0)
    edges = jnp.concatenate([line_ref[0:1], line_ref[slab + 1 : slab + 2]], axis=0)
    for x, plane in zip((0, slab + 1), hartley_plane_pass(edges, right_ref[...], left_ref[...])):
        place(x, plane)

    def lower(x):
        return pltpu.roll(x, 1, 1)

    def upper(x):
        return pltpu.roll(x, width - 1, 1)

    pairs = ((0, 0), (1, 1), (2, 2), (0, 1), (0, 2), (1, 2))

    def contract(x, sums):
        sums = list(sums)
        for block in range(width // ROWS):

            def at(plane, shift):
                return field_ref[plane, PAD + block * ROWS + shift : PAD + (block + 1) * ROWS + shift, :]

            here, south, north = at(x + 1, 0), at(x + 1, -1), at(x + 1, 1)
            east, east_south = at(x + 2, 0), at(x + 2, -1)
            west, west_north = at(x, 0), at(x, 1)
            value = conduct_ref[x, block * ROWS : (block + 1) * ROWS, :]
            in_y, next_y = here - south, north - here
            out_x, into_x = east - here, here - west
            yy = next_y - in_y
            zz = (upper(here) - here) - (here - lower(here))
            second = [
                [mean - value - yy - zz, (east - east_south) - in_y, out_x - lower(out_x)],
                [next_y - (west_north - west), yy, next_y - lower(next_y)],
                [upper(into_x) - into_x, upper(in_y) - in_y, zz],
            ]
            weighted = [[value * second[e][d] for d in range(3)] for e in range(3)]
            for i, (d, f) in enumerate(pairs):
                product = sum(weighted[e][d] * second[e][f] for e in range(3))
                sums[i] = sums[i] + fold(product)
                sums[6 + i] = sums[6 + i] + fold(weighted[f][d])
        return tuple(sums)

    sums = lax.fori_loop(0, slab, contract, (zero,) * 12)
    tiles = [total, square, *sums, zero, zero]
    part_ref[pencil] = jnp.concatenate(
        [jnp.sum(tile, axis=0, keepdims=True) for tile in tiles], axis=0
    )
    part_copies = ring(
        "pencil", pencil, slabs, part_ref.at[pencil], lambda k: part_ref.at[pencil], part_send, part_recv
    )
    for copy in part_copies:
        copy.start()
    for copy in info_copies:
        copy.wait()
    theta = sum(info_ref[k, 4:5, :] for k in range(groups))
    target = sum(info_ref[k, 5:6, :] for k in range(groups))
    for copy in part_copies:
        copy.wait_send()
    for k in range(1, slabs):
        origin = lax.rem(pencil - k + slabs, slabs)
        pltpu.make_async_remote_copy(
            src_ref=part_ref.at[pencil],
            dst_ref=part_ref.at[origin],
            send_sem=part_send.at[k],
            recv_sem=part_recv.at[k],
            device_id={"pencil": origin},
            device_id_type=MESH,
        ).wait_recv()
    whole = sum(part_ref[s] for s in range(slabs))
    stat_ref[0] = jnp.zeros((STATS, 128), F32) + jnp.sum(whole, axis=1, keepdims=True)
    stat_copies = ring(
        "macro", macro, groups, stat_ref.at[0], lambda k: stat_ref.at[k], stat_send, stat_recv
    )
    for copy in stat_copies:
        copy.start()
    for copy in stat_copies:
        copy.wait()

    owners = [lax.rem(macro - k + groups, groups).astype(F32) for k in range(groups)]
    nodes = jnp.zeros((1, 128), F32)
    for q in range(groups):
        weights = info_ref[q]
        local = jnp.zeros((8, 128), F32) + jnp.sum(weights * theta, axis=1, keepdims=True)
        gradient = [local[d : d + 1] for d in range(3)]
        radiative = local[3:4] * local[3:4] * local[3:4]
        choice = weights[6:7]
        stats = jnp.zeros((STATS, 128), F32)
        for k in range(groups):
            stats = stats + jnp.where(choice == owners[k], stat_ref[k], 0.0)
        stats = stats * (1.0 / volume)
        average = stats[0:1]
        square_mean = stats[1:2] + 2.0 * radiative * average + radiative * radiative
        reference_k = jnp.sqrt(square_mean)
        factor = radiative - 2.0 * reference_k
        response = {}
        for i, (d, f) in enumerate(pairs):
            value = (stats[2 + i : 3 + i] - factor * stats[8 + i : 9 + i]) / square_mean
            response[d, f] = response[f, d] = value
        for d in range(3):
            flux = (average + radiative) * gradient[d]
            flux = flux + sum(response[d, e] * gradient[e] for e in range(3))
            nodes = nodes + flux * weights[d : d + 1]
            if q == 0:
                out_ref[d : d + 1, :] = flux
    for n in range(owned):
        wanted = (macro * owned + n + 1).astype(F32)
        row = jnp.sum(jnp.where(target == wanted, nodes, 0.0), axis=1, keepdims=True)
        out_ref[3 + n : 4 + n, :] = jnp.zeros((1, 128), F32) + row


def on_device(right, left, modes, groups, slabs, ids, fiber, phases, theta, corners, positions, choices):
    slab, width = fiber.shape[1], fiber.shape[3]
    owned = theta.shape[0]
    assert corners.shape[0] == 1 and groups * owned <= 128
    rows = -(-(3 + owned) // 8) * 8
    vmem = pl.BlockSpec(memory_space=pltpu.VMEM)
    whole = pl.BlockSpec(memory_space=pltpu.HBM)
    dma = pltpu.SemaphoreType.DMA
    out = pl.pallas_call(
        kernel,
        out_shape=jax.ShapeDtypeStruct((rows, 128), F32),
        in_specs=[whole] * 10,
        out_specs=vmem,
        scratch_shapes=[
            pltpu.SMEM(phases.shape, F32),
            pltpu.SMEM(theta.shape, F32),
            pltpu.SMEM(corners.shape, jnp.int32),
            pltpu.SMEM(positions.shape, jnp.int32),
            pltpu.SMEM(choices.shape, jnp.int32),
            pltpu.VMEM(right.shape, BF16),
            pltpu.VMEM(left.shape, BF16),
            pltpu.VMEM(modes.shape, F32),
            pltpu.VMEM((slab, width, width), jnp.int32),
            pltpu.VMEM((slab, width, width), F32),
            pltpu.VMEM((slab, width, width), F32),
            pltpu.VMEM((slab + 2, width, width), F32),
            pltpu.VMEM((slab + 2, width + 2 * PAD, width), F32),
            pltpu.VMEM((slabs, 2, width, width), F32),
            pltpu.VMEM((groups, 8, 128), F32),
            pltpu.VMEM((slabs, STATS, 128), F32),
            pltpu.VMEM((groups, STATS, 128), F32),
            dma((8,)),
            dma((2, slab // GROUP)),
            dma((slabs,)),
            dma((slabs,)),
            dma((groups,)),
            dma((groups,)),
            dma((slabs,)),
            dma((slabs,)),
            dma((groups,)),
            dma((groups,)),
        ],
        compiler_params=pltpu.CompilerParams(
            collective_id=0, has_side_effects=True, vmem_limit_bytes=60 << 20
        ),
    )(ids, fiber, phases, theta, corners, positions, choices, right, left, modes)
    return out[:3, 0].reshape(1, 3), out[3 : 3 + owned, 0]


def solution(mesh):
    groups, slabs = mesh.shape["macro"], mesh.shape["pencil"]
    in_specs = (
        P("macro", "pencil", None, None),
        P("macro", "pencil", None, None),
        P("macro", None),
        P("macro"),
        P("macro", None),
        P("macro"),
        P("macro"),
    )
    out_specs = (P("macro", None), P("macro"))

    def run(ids, fiber, *rest):
        width = fiber.shape[3]
        right, left = hartley_tables(width)
        modes = mode_tables(width, fiber.shape[1] // slabs)
        body = functools.partial(
            on_device, jnp.asarray(right), jnp.asarray(left), jnp.asarray(modes), groups, slabs
        )
        return jax.shard_map(
            body, mesh=mesh, in_specs=in_specs, out_specs=out_specs, check_vma=False
        )(ids, fiber, *rest)

    return run
```
